128 devices in a mesh: pipe: 4 (over z), seq: 16 (over y, x), cfg: 2 (over core).
Axes of the slice: x: 4, y: 4, z: 4, core: 2. Of those that a mesh axis runs over, the one named last changes fastest.
Arguments:
- hidden: bfloat16 [2, 4, 2048, 5120], P('cfg', 'pipe', 'seq'), may hold values from -6 to 6
- qkv_weight: bfloat16 [4, 5120, 3, 4096], P('pipe', None, None, 'seq'), may hold values from -1 to 1
- out_weight: bfloat16 [4, 4096, 5120], P('pipe', 'seq'), may hold values from -0.09375 to 0.09375
- qk_gain: float32 [4, 2, 4096], P('pipe', None, 'seq'), may hold values from 0 to 8
- stale_kv: bfloat16 [2, 4, 2, 4096, 4096], P('cfg', 'pipe', None, None, 'seq'), may hold values from -6 to 6
- modulation: float32 [4, 50, 3, 5120], P('pipe'), may hold values from -3 to 3
- head_mod: float32 [50, 2, 5120], replicated, may hold values from -3 to 3
- head_weight: bfloat16 [5120, 64], replicated, may hold values from -0.078125 to 0.078125
- patch_index: int32 [1], replicated, may hold values from 0 to 1
- timestep: int32 [1], replicated, may hold values from 0 to 49
Outputs:
- forwarded: bfloat16 [2, 4, 2048, 5120], P('cfg', 'pipe', 'seq')
- fresh_kv: bfloat16 [2, 4, 2, 2048, 4096], P('cfg', 'pipe', None, None, 'seq')
- guided: float32 [4, 2048, 64], P('pipe', 'seq', 'cfg')
The draws below stay inside these ranges and needn't reach their ends.
All inputs are finite; a program needn't handle non-finite values.
Results may differ from the reference program's by a relative error of at most 0.01.
Values may be sent and summed in bfloat16 or wider, within the bound.
No kernel may reach another device: no remote copies, remote signals or barrier semaphores. Data moves between devices by JAX's collectives and lax.ppermute only.
A program may use at most 128 MiB of HBM per device.

```python
import math
import jax
import jax.numpy as jnp
from jax import lax

D = 5120
HEADS = 32
HEAD = 128
OUT_CH = 64
STEPS = 50
NPATCH = 2
PT = 2048
HD = 4096
SEQLEN = 4096
N_PIPE = 4
N_SEQ = 16


def chosen_heads(key):
    return jax.random.randint(jax.random.fold_in(key, 7), (N_PIPE,), 0, HEADS)


def chosen_columns(key):
    heads = chosen_heads(key)
    column_head = jnp.arange(HD, dtype=jnp.int32) // HEAD
    return (column_head[None, :] == heads[:, None]).astype(jnp.float32)


def draw_qkv_weight(key, part):
    base = jnp.clip(jax.random.normal(jax.random.fold_in(key, 11), (N_PIPE, D, 3, HD), jnp.float32), -6.0, 6.0)
    marked = chosen_columns(key)[:, None, :]
    query_cols = base[:, :, 0, :]
    tied = (query_cols + 0.25 * base[:, :, 1, :]) * (1.0 / math.sqrt(1.0625))
    key_cols = marked * tied + (1.0 - marked) * base[:, :, 1, :]
    stacked = jnp.stack([query_cols, key_cols, base[:, :, 2, :]], axis=2)
    return (stacked * D ** (-0.5)).astype(jnp.bfloat16)


def draw_qk_gain(key, part):
    first = jax.random.fold_in(key, 13)
    second = jax.random.fold_in(key, 14)
    third = jax.random.fold_in(key, 15)
    gains = 1.0 + 0.15 * jnp.clip(jax.random.normal(first, (N_PIPE, 2, HD), jnp.float32), -5.0, 5.0)
    level = jnp.exp(jax.random.uniform(second, (N_PIPE, 1, 1), jnp.float32, math.log(4.0), math.log(6.0)))
    ripple = 1.0 + 0.1 * jnp.clip(jax.random.normal(third, (N_PIPE, 2, HD), jnp.float32), -3.0, 3.0)
    marked = chosen_columns(key)[:, None, :]
    return marked * level * ripple + (1.0 - marked) * gains


def draw_hidden(key, part):
    first = jax.random.fold_in(key, 17)
    shape = (2, N_PIPE, PT, D)
    return jnp.clip(jax.random.normal(first, shape, jnp.float32), -6.0, 6.0).astype(jnp.bfloat16)


def level_of(key, dims, cuts, smallest, largest):
    level, own = 1.0, jax.random.fold_in(key, 6)
    for axis_at, parts in cuts:
        heights = jnp.exp(jax.random.uniform(jax.random.fold_in(own, axis_at), (parts,), jnp.float32, smallest / len(cuts), largest / len(cuts)))
        level = level * jnp.repeat(heights, dims[axis_at] // parts).reshape([-1 if axis == axis_at else 1 for axis in range(len(dims))])
    return level


def scatter_about(own_key, dims, width, most, pieces=(), held_as=jnp.bfloat16):
    drawn = jax.random.normal(own_key, dims, jnp.float32) * width
    if len(pieces) > 0:
        drawn = level_of(own_key, dims, pieces, -0.22, 0.18) * drawn
    return jnp.clip(drawn, min=-most, max=most).astype(held_as)


def setup_inputs(seed: int = 0) -> dict:
    splits = jax.random.split(jax.random.key(seed), 11)
    hidden = draw_hidden(jax.random.fold_in(splits[10], 71), 0)
    qkv_weight = draw_qkv_weight(jax.random.fold_in(splits[10], 71), 0)
    out_weight = scatter_about(splits[2], (N_PIPE, HD, D), HD ** -0.5, 0.09375, ((0, 4), (1, 16)))
    qk_gain = draw_qk_gain(jax.random.fold_in(splits[10], 71), 0)
    stale_kv = scatter_about(splits[4], (2, N_PIPE, 2, SEQLEN, HD), 1.0, 6.0, ((0, 2), (1, 4), (4, 16)))
    modulation = scatter_about(splits[5], (N_PIPE, STEPS, 3, D), 0.5, 3.0, ((0, 4),), jnp.float32)
    head_mod = scatter_about(splits[6], (STEPS, 2, D), 0.5, 3.0, (), jnp.float32)
    head_weight = scatter_about(splits[7], (D, OUT_CH), D ** -0.5, 0.078125)
    patch_index = jax.random.randint(splits[8], (1,), 0, NPATCH).astype(jnp.int32)
    timestep = jax.random.randint(splits[9], (1,), 0, STEPS).astype(jnp.int32)
    return {"hidden": hidden, "qkv_weight": qkv_weight, "out_weight": out_weight, "qk_gain": qk_gain, "stale_kv": stale_kv, "modulation": modulation, "head_mod": head_mod, "head_weight": head_weight, "patch_index": patch_index, "timestep": timestep}


epsilon = 1e-06
guidance = 5.0

def modulate(inputs, shift_row, scale_row):
    values = inputs.astype(jnp.float32)
    center = lax.optimization_barrier(jnp.mean(values, axis=-1, keepdims=True))
    spread = lax.optimization_barrier(jnp.mean(jnp.square(values - center), axis=-1, keepdims=True))
    return (values - center) * lax.rsqrt(spread + epsilon) * (1.0 + scale_row) + shift_row

def attend_head(operands):
    queries, key_rows, value_rows = operands
    scores = jnp.dot(queries, key_rows.T, preferred_element_type=jnp.float32) * HEAD ** (-0.5)
    top = lax.optimization_barrier(jnp.max(scores, axis=-1, keepdims=True))
    expo = jnp.exp(scores - top)
    weights = (expo / lax.optimization_barrier(jnp.sum(expo, axis=-1, keepdims=True))).astype(jnp.bfloat16)
    return jnp.dot(weights, value_rows, preferred_element_type=jnp.float32).astype(jnp.bfloat16)

def add_group(carry, operands):
    attn_part, weight_part = operands
    term = jnp.dot(attn_part, weight_part, preferred_element_type=jnp.float32).astype(jnp.bfloat16)
    term = lax.optimization_barrier(term)
    return (carry + term.astype(jnp.float32), None)

def run_section(inputs, qkv_rows, out_rows, qk_gains, stale_pair, mod_rows, patch_slot):
    tokens = inputs.shape[0]
    normed = modulate(inputs, mod_rows[0], mod_rows[1]).astype(jnp.bfloat16)
    projections = jnp.dot(normed, qkv_rows.reshape(D, 3 * HD), preferred_element_type=jnp.float32)
    queries = projections[:, :HD]
    key_cols = projections[:, HD:2 * HD]
    value_cols = projections[:, 2 * HD:]
    query_scale = lax.rsqrt(lax.optimization_barrier(jnp.mean(jnp.square(queries), axis=-1, keepdims=True)) + epsilon)
    key_scale = lax.rsqrt(lax.optimization_barrier(jnp.mean(jnp.square(key_cols), axis=-1, keepdims=True)) + epsilon)
    query_normed = (queries * query_scale * qk_gains[0]).astype(jnp.bfloat16)
    key_normed = (key_cols * key_scale * qk_gains[1]).astype(jnp.bfloat16)
    value_normed = value_cols.astype(jnp.bfloat16)
    first_row = (patch_slot * tokens).astype(jnp.int32)
    key_set = lax.dynamic_update_slice(stale_pair[0], key_normed, (first_row, jnp.int32(0)))
    value_set = lax.dynamic_update_slice(stale_pair[1], value_normed, (first_row, jnp.int32(0)))
    query_heads = query_normed.reshape(tokens, HEADS, HEAD).transpose(1, 0, 2)
    key_heads = key_set.reshape(SEQLEN, HEADS, HEAD).transpose(1, 0, 2)
    value_heads = value_set.reshape(SEQLEN, HEADS, HEAD).transpose(1, 0, 2)
    attended = lax.map(attend_head, (query_heads, key_heads, value_heads))
    attended = attended.transpose(1, 0, 2).reshape(tokens, HD)
    group_width = HD // N_SEQ
    attn_groups = attended.reshape(tokens, N_SEQ, group_width).transpose(1, 0, 2)
    weight_groups = out_rows.reshape(N_SEQ, group_width, D)
    projected, _ = lax.scan(add_group, jnp.zeros((tokens, D), jnp.float32), (attn_groups, weight_groups))
    result = (inputs.astype(jnp.float32) + mod_rows[2] * projected).astype(jnp.bfloat16)
    return (result, jnp.stack([key_normed, value_normed]))

def reference(hidden, qkv_weight, out_weight, qk_gain, stale_kv, modulation, head_mod, head_weight, patch_index, timestep):
    step_row = timestep[0]
    head_rows = lax.dynamic_index_in_dim(head_mod, step_row, 0, keepdims=False)
    results = []
    fresh_all = []
    readouts = []
    for branch in range(2):
        branch_results = []
        branch_fresh = []
        branch_reads = []
        for section_index in range(N_PIPE):
            mod_rows = lax.dynamic_index_in_dim(modulation[section_index], step_row, 0, keepdims=False)
            patch_slot = jnp.mod(patch_index[0] - section_index, NPATCH)
            result, fresh_pair = run_section(hidden[branch, section_index], qkv_weight[section_index], out_weight[section_index], qk_gain[section_index], stale_kv[branch, section_index], mod_rows, patch_slot)
            normed_out = modulate(result, head_rows[0], head_rows[1]).astype(jnp.bfloat16)
            branch_reads.append(jnp.dot(normed_out, head_weight, preferred_element_type=jnp.float32))
            branch_results.append(result)
            branch_fresh.append(fresh_pair)
        results.append(branch_results)
        fresh_all.append(jnp.stack(branch_fresh))
        readouts.append(branch_reads)
    forwarded = jnp.stack([jnp.stack([results[branch][(section_index - 1) % N_PIPE] for section_index in range(N_PIPE)]) for branch in range(2)])
    fresh_kv = jnp.stack(fresh_all)
    guided = jnp.stack([readouts[1][section_index] + guidance * (readouts[0][section_index] - readouts[1][section_index]) for section_index in range(N_PIPE)])
    return (forwarded, fresh_kv, guided)
```

```python
import math

import jax
import jax.numpy as jnp
from jax import lax
from jax.experimental import pallas as pl
from jax.experimental.pallas import tpu as pltpu
from jax.sharding import PartitionSpec as P

HEAD = 128
NPATCH = 2
SIDE = 4
CHUNKS = 2

epsilon = 1e-06
guidance = 5.0


def passed_along(block, axis, distance):
    devices = range(lax.axis_size(axis))
    route = [((i - distance) % len(devices), i) for i in devices]
    return lax.ppermute(block, axis, route)


def along_x(block, distance):
    route = [(y * SIDE + x, y * SIDE + (x + distance) % SIDE) for y in range(SIDE) for x in range(SIDE)]
    return lax.ppermute(block, "seq", route)


def along_y(block, distance):
    route = [(y * SIDE + x, (y + distance) % SIDE * SIDE + x) for y in range(SIDE) for x in range(SIDE)]
    return lax.ppermute(block, "seq", route)


def partner_2(shard, axis, stride):
    return lax.ppermute(shard, axis, [(i, i ^ 1 << stride) for i in range(lax.axis_size(axis))])


def plane_sum(values):
    for shift in (along_x, along_y):
        parts = [values] + [shift(values, d) for d in range(1, SIDE)]
        values = (parts[0] + parts[2]) + (parts[1] + parts[3])
    return values


def modulate(inputs, shift_row, scale_row):
    values = inputs.astype(jnp.float32)
    center = jnp.mean(values, axis=-1, keepdims=True)
    spread = jnp.mean(jnp.square(values - center), axis=-1, keepdims=True)
    return (values - center) * lax.rsqrt(spread + epsilon) * (1.0 + scale_row) + shift_row


def norm_kernel(*refs):
    projections, scales = refs[:CHUNKS], refs[CHUNKS : 2 * CHUNKS]
    gain_ref, q_ref, kv_ref = refs[2 * CHUNKS :]
    width = q_ref.shape[-1]
    for c in range(CHUNKS):
        proj, scale = projections[c], scales[c]
        q_ref[0, c] = (proj[0, :, :width] * scale[0, :, 0:1] * gain_ref[0:1]).astype(jnp.bfloat16)
        kv_ref[0, 0, c] = (proj[0, :, width : 2 * width] * scale[0, :, 1:2] * gain_ref[1:2]).astype(jnp.bfloat16)
        kv_ref[1, 0, c] = proj[0, :, 2 * width :].astype(jnp.bfloat16)


def normalize(projections, scales, gains):
    owners, rows, width3 = projections[0].shape
    width = width3 // 3
    return pl.pallas_call(
        norm_kernel,
        grid=(owners,),
        in_specs=[pl.BlockSpec((1, rows, width3), lambda i: (i, 0, 0))] * CHUNKS
        + [pl.BlockSpec((1, rows, 2), lambda i: (i, 0, 0))] * CHUNKS
        + [pl.BlockSpec((2, width), lambda i: (0, 0))],
        out_specs=[
            pl.BlockSpec((1, CHUNKS, rows, width), lambda i: (i, 0, 0, 0)),
            pl.BlockSpec((2, 1, CHUNKS, rows, width), lambda i: (0, i, 0, 0, 0)),
        ],
        out_shape=[
            jax.ShapeDtypeStruct((owners, CHUNKS, rows, width), jnp.bfloat16),
            jax.ShapeDtypeStruct((2, owners, CHUNKS, rows, width), jnp.bfloat16),
        ],
    )(*projections, *scales, gains)


KEY_STEP = 1024


def attend_kernel(other_ref, q_ref, ks_ref, vs_ref, kf_ref, vf_ref, o_ref):
    queries = q_ref[...]
    rows = queries.shape[0]
    factor = HEAD ** (-0.5) * math.log2(math.e)
    half = kf_ref.shape[-2]
    steps = [(k, v, pl.ds(at, KEY_STEP)) for k, v in ((ks_ref, vs_ref), (kf_ref, vf_ref)) for at in range(0, half, KEY_STEP)]

    def scores_of(step):
        keys = step[0][step[2], :]
        return lax.dot_general(queries, keys, (((1,), (1,)), ((), ())), preferred_element_type=jnp.float32)

    scores = scores_of(steps[0])
    top, total, mixed = None, None, None
    for n, step in enumerate(steps):
        later = scores_of(steps[n + 1]) if n + 1 < len(steps) else None
        peak = jnp.max(scores, axis=-1, keepdims=True)
        new_top = peak if top is None else jnp.maximum(top, peak)
        expo = jnp.exp2((scores - new_top) * factor)
        weight_sum = jnp.sum(expo, axis=-1, keepdims=True)
        part = jnp.dot(expo.astype(jnp.bfloat16), step[1][step[2], :], preferred_element_type=jnp.float32)
        if top is None:
            total, mixed = weight_sum, part
        else:
            fade = jnp.exp2((top - new_top) * factor)
            total, mixed = total * fade + weight_sum, mixed * fade + part
        top, scores = new_top, later
    o_ref[...] = (mixed / total).astype(jnp.bfloat16)


def attend(queries, stale, fresh, other, block_rows):
    rows, width = queries.shape
    half = fresh.shape[3]
    heads = width // HEAD
    kv_block = (1, 1, 1, half, HEAD)
    grid_spec = pltpu.PrefetchScalarGridSpec(
        num_scalar_prefetch=1,
        grid=(heads, rows // block_rows),
        in_specs=[
            pl.BlockSpec((block_rows, HEAD), lambda h, i, o: (i, h)),
            pl.BlockSpec(kv_block, lambda h, i, o: (0, 0, 0, o[0], h)),
            pl.BlockSpec(kv_block, lambda h, i, o: (0, 0, 1, o[0], h)),
            pl.BlockSpec(kv_block, lambda h, i, o: (0, 0, 0, 0, h)),
            pl.BlockSpec(kv_block, lambda h, i, o: (0, 0, 1, 0, h)),
        ],
        out_specs=pl.BlockSpec((block_rows, HEAD), lambda h, i, o: (i, h)),
    )
    return pl.pallas_call(
        attend_refs,
        grid_spec=grid_spec,
        out_shape=jax.ShapeDtypeStruct((rows, width), jnp.bfloat16),
        cost_estimate=pl.CostEstimate(
            flops=8 * rows * half * width, bytes_accessed=20 * half * width, transcendentals=2 * rows * half * heads
        ),
    )(other, queries, stale, stale, fresh, fresh)


def attend_refs(other_ref, q_ref, ks_ref, vs_ref, kf_ref, vf_ref, o_ref):
    attend_kernel(other_ref, q_ref, *(r.at[0, 0, 0] for r in (ks_ref, vs_ref, kf_ref, vf_ref)), o_ref)


def project_kernel(*refs):
    parts, weights, o_ref = refs[:SIDE], refs[SIDE : 2 * SIDE], refs[2 * SIDE]
    total = None
    for part, weight in zip(parts, weights):
        term = jnp.dot(part[...], weight[...], preferred_element_type=jnp.float32)
        total = term if total is None else total + term
    o_ref[...] = total.astype(jnp.bfloat16)


def project(parts, weights, tile):
    rows, depth = parts[0].shape
    columns = weights[0].shape[1]
    return pl.pallas_call(
        project_kernel,
        grid=(columns // tile,),
        in_specs=[pl.BlockSpec((rows, depth), lambda j: (0, 0))] * SIDE
        + [pl.BlockSpec((depth, tile), lambda j: (0, j))] * SIDE,
        out_specs=pl.BlockSpec((rows, tile), lambda j: (0, j)),
        out_shape=jax.ShapeDtypeStruct((rows, columns), jnp.bfloat16),
        cost_estimate=pl.CostEstimate(
            flops=2 * rows * depth * SIDE * columns, bytes_accessed=2 * SIDE * depth * (rows + columns), transcendentals=0
        ),
    )(*parts, *weights)


def per_device(
    hidden,
    qkv_weight,
    out_weight,
    qk_gain,
    stale_kv,
    modulation,
    head_mod,
    head_weight,
    patch_index,
    timestep,
):
    tokens_in = hidden[0, 0]
    own_rows, model_width = tokens_in.shape
    step_row = timestep[0]
    mod_rows = lax.dynamic_index_in_dim(modulation[0], step_row, 0, keepdims=False)
    head_rows = lax.dynamic_index_in_dim(head_mod, step_row, 0, keepdims=False)
    in_weight = qkv_weight[0]
    width = in_weight.shape[2]
    in_weight = in_weight.reshape(model_width, 3 * width)
    devices = lax.axis_size("seq")
    full_width = width * devices
    place = lax.axis_index("seq")
    here_x, here_y = place % SIDE, place // SIDE

    half_model = model_width // 2
    weight_x, weight_y = out_weight[0, :, :half_model], out_weight[0, :, half_model:]
    weights_x = [weight_x] + [along_x(weight_x, d) for d in range(1, SIDE)]
    weights_y = [weight_y] + [along_y(weight_y, d) for d in range(1, SIDE)]

    normed = modulate(tokens_in, mod_rows[0], mod_rows[1]).astype(jnp.bfloat16)
    chunk_rows = own_rows // CHUNKS
    gathered = [
        lax.all_gather(normed[c * chunk_rows : (c + 1) * chunk_rows], "seq", axis=0, tiled=True) for c in range(CHUNKS)
    ]
    projections, scales = [], []
    for chunk in gathered:
        projected = jnp.dot(chunk, in_weight, preferred_element_type=jnp.float32)
        squares = jnp.stack(
            [jnp.sum(jnp.square(projected[:, n * width : (n + 1) * width]), axis=-1) for n in range(2)]
        )
        scale = lax.rsqrt(plane_sum(squares) / full_width + epsilon)
        projections.append(projected.reshape(devices, chunk_rows, 3 * width))
        scales.append(scale.T.reshape(devices, chunk_rows, 2))
    query_normed, fresh = normalize(projections, scales, qk_gain[0])
    tokens = devices * own_rows
    query_normed = query_normed.reshape(tokens, width)
    fresh = fresh.reshape(1, 1, 2, tokens, width)
    patch_slot = jnp.mod(patch_index[0] - lax.axis_index("pipe"), NPATCH)
    other = (1 - patch_slot).astype(jnp.int32).reshape(1)
    attended = attend(query_normed, stale_kv, fresh, other, 512)

    grid = attended.reshape(SIDE, SIDE, own_rows, width)

    def for_x(d):
        block = lax.dynamic_index_in_dim(grid, (here_x + d) % SIDE, 1, keepdims=False)
        return block.reshape(SIDE * own_rows, width)

    def for_y(d):
        block = lax.dynamic_index_in_dim(grid, (here_y + d) % SIDE, 0, keepdims=False)
        return block.reshape(SIDE * own_rows, width)

    parts_x = [for_x(0)] + [along_x(for_x(d), d) for d in range(1, SIDE)]
    parts_y = [for_y(0)] + [along_y(for_y(d), d) for d in range(1, SIDE)]
    terms_x = project(parts_x, weights_x, 512).reshape(SIDE, own_rows, half_model)
    terms_y = project(parts_y, weights_y, 512).reshape(SIDE, own_rows, half_model)

    def scattered(terms, here, shift):
        own = [lax.dynamic_index_in_dim(terms, (here + d) % SIDE, 0, keepdims=False) for d in range(SIDE)]
        moved = [own[0]] + [shift(own[d], d) for d in range(1, SIDE)]
        moved = [part.astype(jnp.float32) for part in moved]
        return (moved[0] + moved[2]) + (moved[1] + moved[3])

    halves = []
    for n, sums in enumerate((scattered(terms_x, here_y, along_y), scattered(terms_y, here_x, along_x))):
        cut = slice(n * half_model, (n + 1) * half_model)
        halves.append((tokens_in[:, cut].astype(jnp.float32) + mod_rows[2, cut] * sums).astype(jnp.bfloat16))
    forwarded = jnp.concatenate([passed_along(half, "pipe", 1) for half in halves], axis=1)
    block_out = jnp.concatenate(halves, axis=1)
    normed_out = modulate(block_out, head_rows[0], head_rows[1]).astype(jnp.bfloat16)
    readout = jnp.dot(normed_out, head_weight, preferred_element_type=jnp.float32)
    branch_index = lax.axis_index("cfg")
    half_width = readout.shape[1] // 2
    partner = partner_2(readout.astype(jnp.bfloat16), "cfg", 0).astype(readout.dtype)
    conditional = jnp.where(branch_index == 0, readout, partner)
    unconditional = jnp.where(branch_index == 0, partner, readout)
    combined = unconditional + guidance * (conditional - unconditional)
    guided = lax.dynamic_slice_in_dim(combined, branch_index * half_width, half_width, 1)
    return (forwarded[None, None], fresh, guided[None])


def solution(mesh):
    return jax.shard_map(
        per_device,
        mesh=mesh,
        in_specs=(
            P("cfg", "pipe", "seq", None),
            P("pipe", None, None, "seq"),
            P("pipe", "seq", None),
            P("pipe", None, "seq"),
            P("cfg", "pipe", None, None, "seq"),
            P("pipe", None, None, None),
            P(),
            P(),
            P(),
            P(),
        ),
        out_specs=(
            P("cfg", "pipe", "seq", None),
            P("cfg", "pipe", None, None, "seq"),
            P("pipe", "seq", "cfg"),
        ),
        check_vma=False,
    )
```
